32 devices in a mesh: band: 2 (over x), col: 16 (over z, y, core).
Axes of the slice: x: 2, y: 2, z: 4, core: 2. Of those that a mesh axis runs over, the one named last changes fastest.
Arguments:
- fields: bfloat16 [4, 80, 16, 2048], P(None, None, 'band', 'col'), may hold values from -6 to 6
- inverse: bfloat16 [4, 80, 80], replicated, may hold values from -1 to 2
- block_costs: int32 [16, 16], P('col', 'band'), may hold values from 1 to 8, as said below
- row_length: int32 [16], P('band'), may hold values from 1025 to 2048
Outputs:
- spectra: float32 [320, 16, 2, 512], P('col', None, None, 'band')
The draws below stay inside these ranges and needn't reach their ends.
Inputs may be any that keep to these rules, and one draw needn't show every extreme that they name: `block_costs`: at least one block takes 8 substeps and at least one takes 1.
All inputs are finite; a program needn't handle non-finite values.
Results may differ from the reference program's by a relative error of at most 0.0042.
Values may be sent and summed in bfloat16 or wider, within the bound.
A program may use at most 64 MiB of HBM per device.

```python
import math
import jax
import jax.numpy as jnp
from jax import lax

FIELDS = 4
LEV = 80
BLOCK = 128
CMAX = 8
ROWS = 16
NLON = 2048
WAVES = 512
N_COL = 16


def draw_inverse(key, part):
    key_diag, key_off = jax.random.split(jax.random.fold_in(key, 11))
    diagonal_part = 0.5 + 0.4 * jax.random.uniform(key_diag, (FIELDS, LEV), jnp.float32)
    off_part = jnp.clip(jax.random.normal(key_off, (FIELDS, LEV, LEV), jnp.float32), -1.7, 1.7) * 0.35
    off_part = off_part / jnp.sqrt(jnp.float32(LEV))
    identity = jnp.eye(LEV, dtype=jnp.float32)
    return (off_part + diagonal_part[:, :, None] * identity[None, :, :]).astype(jnp.bfloat16)


def draw_block_costs(key, part):
    key_heavy, key_cost = jax.random.split(jax.random.fold_in(key, 23))
    heavy_mask = jax.random.randint(key_heavy, (N_COL, 1), 0, 4) == 0
    top_cost = jnp.where(heavy_mask, CMAX, 1).astype(jnp.int32)
    costs_drawn = 1 + jax.random.randint(key_cost, (N_COL, ROWS), 0, top_cost)
    costs_drawn = costs_drawn.at[0, 0].set(CMAX).at[0, 1].set(1)
    return costs_drawn.astype(jnp.int32)


def set_ends(drawn, own_key, low, top_value):
    place = [jax.random.randint(jax.random.fold_in(own_key, axis), (), 0, length) for axis, length in enumerate(drawn.shape)]
    main_axis = drawn.shape.index(max(drawn.shape))
    next_to = place[:main_axis] + [(place[main_axis] + 1) % drawn.shape[main_axis]] + place[main_axis + 1:]
    return drawn.at[tuple(place)].set(low).at[tuple(next_to)].set(top_value)


def block_scale(stream_key, extent, cuts, smallest, largest):
    loudness, own = 1.0, jax.random.fold_in(stream_key, 6)
    for axis_at, shards_of in cuts:
        steps = jnp.exp(jax.random.uniform(jax.random.fold_in(own, axis_at), (shards_of,), jnp.float32, smallest / len(cuts), largest / len(cuts)))
        loudness = loudness * jnp.repeat(steps, extent[axis_at] // shards_of).reshape([-1 if axis == axis_at else 1 for axis in range(len(extent))])
    return loudness


def bell_draw(own_key, shape, width, limit, cuts=(), kind=jnp.bfloat16):
    drawn = width * jax.random.normal(own_key, shape, jnp.float32)
    if cuts:
        drawn = drawn * block_scale(own_key, shape, cuts, -0.22, 0.18)
    return jnp.clip(drawn, -limit, limit).astype(kind)


def setup_inputs(seed: int = 0) -> dict:
    key_list = jax.random.split(jax.random.key(seed), 5)
    return {
        "fields": bell_draw(key_list[0], (FIELDS, LEV, ROWS, NLON), 1.0, 6.0, ((2, 2), (3, 16))),
        "inverse": draw_inverse(jax.random.fold_in(key_list[4], 71), 0),
        "block_costs": draw_block_costs(jax.random.fold_in(key_list[4], 71), 0),
        "row_length": set_ends(jax.random.randint(key_list[3], (ROWS,), NLON // 2 + 1, NLON + 1), jax.random.fold_in(key_list[3], 1), NLON // 2 + 1, NLON).astype(jnp.int32),
    }


def reference(fields, inverse, block_costs, row_length):
    inverse_f32 = inverse.astype(jnp.float32)

    def row_spectrum(operands):
        field_row, cost_row, length_row = operands
        initial = field_row.reshape(FIELDS, LEV, N_COL, BLOCK)
        relaxed = initial
        for sweep_index in range(CMAX):
            applied = jnp.einsum('fkl,flcb->fkcb', inverse_f32, relaxed.astype(jnp.float32), precision=lax.Precision.HIGHEST).astype(jnp.bfloat16)
            relaxed = jnp.where((sweep_index < cost_row)[None, None, :, None], applied, relaxed)
        tendency = (relaxed.astype(jnp.float32) - initial.astype(jnp.float32)).astype(jnp.bfloat16)
        tendency = lax.optimization_barrier(tendency)
        updated = (initial.astype(jnp.float32) + tendency.astype(jnp.float32)).astype(jnp.bfloat16)
        updated = updated.reshape(FIELDS * LEV, NLON)
        longitude = jnp.arange(NLON, dtype=jnp.int32)
        masked = jnp.where(longitude[None, :] < length_row, updated, jnp.zeros_like(updated))
        spectrum = jnp.fft.rfft(masked.astype(jnp.float32), axis=-1)[:, :WAVES]
        scale_factor = 1.0 / math.sqrt(NLON)
        parts = jnp.stack([jnp.real(spectrum), jnp.imag(spectrum)], axis=1).astype(jnp.float32)
        return parts * scale_factor
    per_row = lax.map(row_spectrum, (jnp.moveaxis(fields, 2, 0), block_costs.T, row_length))
    return jnp.transpose(per_row, (1, 0, 2, 3))
```

```python
import functools
import math

import jax
import jax.numpy as jnp
import numpy as np
from jax import lax
from jax.experimental import pallas as pl
from jax.experimental.pallas import tpu as pltpu
from jax.sharding import PartitionSpec as P

sweep_total = 8
MESH = pl.DeviceIdType.MESH


def flip(position, step, total):
    result, bit = 0, 1
    while bit < total:
        result = result + bit * (((position // bit) + (step // bit)) % 2)
        bit *= 2
    return result


def relax_kernel(cost_ref, length_ref, fields_ref, inverse_ref, out_ref, start_ref, state_ref, turn_ref):
    field_total, level_total, row_total, width = fields_ref.shape
    first = lax.axis_index("col") * width
    for f in range(field_total):
        turn_ref[f] = fields_ref[f].astype(jnp.float32).reshape(level_total * row_total, width)
    for f in range(field_total):
        for r in range(row_total):
            piece = turn_ref[f, pl.ds(r, level_total, stride=row_total), :].astype(jnp.bfloat16)
            start_ref[f, :, r * width : (r + 1) * width] = piece
            state_ref[f, :, r * width : (r + 1) * width] = piece
    costs = jnp.concatenate(
        [jnp.full((1, width), cost_ref[0, r], jnp.int32) for r in range(row_total)], axis=1
    )

    def sweep(s, carry):
        active = costs > s
        for f in range(field_total):
            before = state_ref[f]
            applied = jnp.dot(inverse_ref[f], before, preferred_element_type=jnp.float32)
            state_ref[f] = jnp.where(active, applied, before.astype(jnp.float32)).astype(jnp.bfloat16)
        return carry

    lax.fori_loop(0, sweep_total, sweep, 0)
    longitude = first + lax.broadcasted_iota(jnp.int32, (1, width), 1)
    for f in range(field_total):
        for r in range(row_total):
            initial = start_ref[f, :, r * width : (r + 1) * width].astype(jnp.float32)
            relaxed = state_ref[f, :, r * width : (r + 1) * width].astype(jnp.float32)
            tendency = (relaxed - initial).astype(jnp.bfloat16)
            updated = (initial + tendency.astype(jnp.float32)).astype(jnp.bfloat16)
            keep = longitude < length_ref[r]
            turn_ref[f, pl.ds(r, level_total, stride=row_total), :] = jnp.where(
                keep, updated.astype(jnp.float32), 0.0
            )
    for f in range(field_total):
        out_ref[f] = turn_ref[f].reshape(level_total, row_total, width).astype(jnp.bfloat16)


def fourier_kernel(
    col_total, band_total, blocks_ref, base_ref, phase_ref, out_ref,
    landed, total, outgoing, incoming, base_buf, send_sem, recv_sem, band_send, band_recv, base_sem,
):
    me, band = lax.axis_index("col"), lax.axis_index("band")
    level_total, row_total, width = landed.shape[1:]
    piece_width = total.shape[2]
    barrier = pltpu.get_barrier_semaphore()
    base_copy = pltpu.make_async_copy(base_ref, base_buf, base_sem)
    base_copy.start()

    def greet(t, carry):
        pl.semaphore_signal(
            barrier, inc=1, device_id={"col": flip(me, t, col_total)}, device_id_type=MESH
        )
        return carry

    lax.fori_loop(1, col_total, greet, 0)
    for j in range(1, band_total):
        pl.semaphore_signal(
            barrier, inc=1, device_id={"band": (band + j) % band_total}, device_id_type=MESH
        )
    pl.semaphore_wait(barrier, col_total - 1 + band_total - 1)

    def block_copy(t):
        peer = flip(me, t, col_total)
        return pltpu.make_async_remote_copy(
            src_ref=blocks_ref.at[peer],
            dst_ref=landed.at[me],
            send_sem=send_sem.at[peer],
            recv_sem=recv_sem.at[me],
            device_id={"col": peer},
            device_id_type=MESH,
        )

    def arrival(t):
        peer = flip(me, t, col_total)
        return pltpu.make_async_remote_copy(
            src_ref=blocks_ref.at[peer],
            dst_ref=landed.at[peer],
            send_sem=send_sem.at[peer],
            recv_sem=recv_sem.at[peer],
            device_id={"col": peer},
            device_id_type=MESH,
        )

    def send(t, carry):
        block_copy(col_total - t).start()
        return carry

    lax.fori_loop(1, col_total, send, 0)
    base_copy.wait()

    def accumulate(block, source, first):
        rows = block.astype(jnp.float32).reshape(level_total * row_total, width).astype(jnp.bfloat16)
        for j in range(band_total):
            lanes = slice(j * piece_width, (j + 1) * piece_width)
            table = (
                base_buf[0, :, lanes] * phase_ref[source, 0:1, lanes]
                + base_buf[1, :, lanes] * phase_ref[source, 1:2, lanes]
            ).astype(jnp.bfloat16)
            value = jnp.dot(rows, table, preferred_element_type=jnp.float32)
            total[j] = value if first else total[j] + value

    accumulate(blocks_ref[me], me, True)

    def receive(t, carry):
        arrival(t).wait_recv()
        source = flip(me, t, col_total)
        accumulate(landed[source], source, False)
        return carry

    lax.fori_loop(1, col_total, receive, 0)

    def band_copy(j, to_peer):
        peer = (band + j) % band_total
        return pltpu.make_async_remote_copy(
            src_ref=outgoing.at[peer],
            dst_ref=incoming.at[band if to_peer else peer],
            send_sem=band_send.at[peer],
            recv_sem=band_recv.at[band if to_peer else peer],
            device_id={"band": peer},
            device_id_type=MESH,
        )

    for j in range(1, band_total):
        peer = (band + j) % band_total
        outgoing[peer] = total[peer].astype(jnp.bfloat16)
    for j in range(1, band_total):
        band_copy(j, True).start()
    shape = (level_total, row_total, piece_width)
    out_ref[:, band] = total[band].reshape(shape)
    for j in range(1, band_total):
        peer = (band + j) % band_total
        band_copy(j, False).wait_recv()
        out_ref[:, peer] = incoming[peer].astype(jnp.float32).reshape(shape)

    def drain(t, carry):
        block_copy(t).wait_send()
        return carry

    lax.fori_loop(1, col_total, drain, 0)
    for j in range(1, band_total):
        band_copy(j, True).wait_send()


def tables(width, col_total, band_total):
    length = width * col_total
    waves = np.arange(length // 4, dtype=np.int64).reshape(band_total, 1, -1)
    wave_of = np.broadcast_to(waves, (band_total, 2, waves.shape[-1])).reshape(-1)
    imaginary = np.broadcast_to(np.arange(2).reshape(1, 2, 1), (band_total, 2, waves.shape[-1])).reshape(-1)
    angle = 2.0 * np.pi * ((np.arange(width)[:, None] * wave_of[None, :]) % length) / length
    cosine, sine = np.cos(angle), np.sin(angle)
    plain = np.where(imaginary[None, :] == 1, -sine, cosine)
    crossed = np.where(imaginary[None, :] == 1, -cosine, -sine)
    base = np.stack([plain, crossed]) / math.sqrt(length)
    turn = 2.0 * np.pi * ((np.arange(col_total)[:, None] * wave_of[None, :]) % col_total) / col_total
    phase = np.stack([np.cos(turn), np.sin(turn)], axis=1)
    return base.astype(np.float32), phase.astype(np.float32)


def shards(fields, inverse, block_costs, row_length):
    field_total, level_total, row_total, width = fields.shape
    col_total, band_total = lax.axis_size("col"), lax.axis_size("band")
    own_levels = field_total * level_total // col_total
    vmem = pl.BlockSpec(memory_space=pltpu.VMEM)
    smem = pl.BlockSpec(memory_space=pltpu.SMEM)
    masked = pl.pallas_call(
        relax_kernel,
        name="relax",
        out_shape=jax.ShapeDtypeStruct(fields.shape, jnp.bfloat16),
        in_specs=[smem, smem, vmem, vmem],
        out_specs=vmem,
        scratch_shapes=[
            pltpu.VMEM((field_total, level_total, row_total * width), jnp.bfloat16),
            pltpu.VMEM((field_total, level_total, row_total * width), jnp.bfloat16),
            pltpu.VMEM((field_total, level_total * row_total, width), jnp.float32),
        ],
    )(block_costs, row_length, fields, inverse)
    blocks = masked.reshape(col_total, own_levels, row_total, width)
    base, phase = tables(width, col_total, band_total)
    own_rows, piece_width = own_levels * row_total, base.shape[2] // band_total
    spectra = pl.pallas_call(
        functools.partial(fourier_kernel, col_total, band_total),
        name="fourier",
        out_shape=jax.ShapeDtypeStruct((own_levels, band_total, row_total, piece_width), jnp.float32),
        in_specs=[vmem, pl.BlockSpec(memory_space=pl.ANY), vmem],
        out_specs=vmem,
        scratch_shapes=[
            pltpu.VMEM((col_total, own_levels, row_total, width), jnp.bfloat16),
            pltpu.VMEM((band_total, own_rows, piece_width), jnp.float32),
            pltpu.VMEM((band_total, own_rows, piece_width), jnp.bfloat16),
            pltpu.VMEM((band_total, own_rows, piece_width), jnp.bfloat16),
            pltpu.VMEM(base.shape, jnp.float32),
            pltpu.SemaphoreType.DMA((col_total,)),
            pltpu.SemaphoreType.DMA((col_total,)),
            pltpu.SemaphoreType.DMA((band_total,)),
            pltpu.SemaphoreType.DMA((band_total,)),
            pltpu.SemaphoreType.DMA,
        ],
        compiler_params=pltpu.CompilerParams(collective_id=0, has_side_effects=True),
    )(blocks, jnp.asarray(base), jnp.asarray(phase))
    return spectra.reshape(own_levels, band_total * row_total, 2, piece_width // 2)


def solution(mesh):
    return jax.shard_map(
        shards,
        mesh=mesh,
        in_specs=(P(None, None, "band", "col"), P(), P("col", "band"), P("band")),
        out_specs=P("col", None, None, "band"),
        check_vma=False,
    )
```

```python
import functools
import math

import jax
import jax.numpy as jnp
import numpy as np
from jax import lax
from jax.experimental import pallas as pl
from jax.experimental.pallas import tpu as pltpu
from jax.sharding import PartitionSpec as P

sweep_total = 8
MESH = pl.DeviceIdType.MESH


def flip(position, step, total):
    result, bit = 0, 1
    while bit < total:
        result = result + bit * (((position // bit) + (step // bit)) % 2)
        bit *= 2
    return result


def spectral_kernel(
    col_total, band_total, scale,
    cost_ref, length_ref, fields_ref, inverse_ref, base_ref, phase_ref, out_ref,
    fields_buf, turn_in, turn_out, state_ref, blocks, landed, total, outgoing, incoming, base_buf,
    field_sem, base_sem, send_sem, recv_sem, band_send, band_recv,
):
    me, band = lax.axis_index("col"), lax.axis_index("band")
    field_total, level_total, row_total, width = fields_buf.shape
    own_levels = landed.shape[1]
    piece_width = total.shape[2]
    group = col_total // field_total
    place, inside = me // group, me % group
    toward = 1 - 2 * (place // (field_total // 2))
    head = (3 * own_levels + 4) // 5
    chunks = ((0, head), (head, own_levels - head))

    def field_of(i):
        return (place + field_total + toward * (1 + i)) % field_total

    def field_copy(i):
        f = field_of(i)
        return pltpu.make_async_copy(fields_ref.at[f], fields_buf.at[i], field_sem.at[i])

    for i in range(field_total):
        field_copy(i).start()
    base_copy = pltpu.make_async_copy(base_ref, base_buf, base_sem)
    base_copy.start()
    barrier = pltpu.get_barrier_semaphore()

    def greet(t, carry):
        pl.semaphore_signal(
            barrier, inc=1, device_id={"col": (me + t) % col_total}, device_id_type=MESH
        )
        return carry

    lax.fori_loop(1, col_total, greet, 0)
    for j in range(1, band_total):
        pl.semaphore_signal(
            barrier, inc=1, device_id={"band": (band + j) % band_total}, device_id_type=MESH
        )

    costs = jnp.concatenate(
        [jnp.full((1, width), cost_ref[0, r], jnp.int32) for r in range(row_total)], axis=1
    )
    longitude = me * width + lax.broadcasted_iota(jnp.int32, (1, width), 1)
    keep = jnp.concatenate(
        [(longitude < length_ref[r]).astype(jnp.int32) for r in range(row_total)], axis=0
    )[None] > 0

    def relax(pair):
        for k in range(2):
            field_copy(2 * pair + k).wait()
            turn_in[k] = (
                fields_buf[2 * pair + k].astype(jnp.float32).reshape(level_total * row_total, width)
            )
        for k in range(2):
            for r in range(row_total):
                piece = turn_in[k, pl.ds(r, level_total, stride=row_total), :]
                state_ref[k, :, r * width : (r + 1) * width] = piece.astype(jnp.bfloat16)

        def sweep(s, carry):
            active = costs > s
            for k in range(2):
                before = state_ref[k]
                applied = jnp.dot(
                    inverse_ref[field_of(2 * pair + k)], before, preferred_element_type=jnp.float32
                )
                state_ref[k] = jnp.where(
                    active, applied, before.astype(jnp.float32)
                ).astype(jnp.bfloat16)
            return carry

        lax.fori_loop(0, sweep_total, sweep, 0)
        for k in range(2):
            for r in range(row_total):
                turn_out[k, pl.ds(r, level_total, stride=row_total), :] = state_ref[
                    k, :, r * width : (r + 1) * width
                ].astype(jnp.float32)
        for k in range(2):
            f = field_of(2 * pair + k)
            for q in range(group):
                rows = slice(q * own_levels * row_total, (q + 1) * own_levels * row_total)
                shape = (own_levels, row_total, width)
                initial = turn_in[k, rows, :].reshape(shape)
                tendency = (turn_out[k, rows, :].reshape(shape) - initial).astype(jnp.bfloat16)
                updated = initial + tendency.astype(jnp.float32)
                blocks[f * group + q] = jnp.where(keep, updated, 0.0).astype(jnp.bfloat16)

    def block_copy(chunk, peer, source):
        start, size = chunks[chunk]
        return pltpu.make_async_remote_copy(
            src_ref=blocks.at[peer, pl.ds(start, size)],
            dst_ref=landed.at[source, pl.ds(start, size)],
            send_sem=send_sem.at[chunk, peer],
            recv_sem=recv_sem.at[chunk, source],
            device_id={"col": peer},
            device_id_type=MESH,
        )

    def send_field(chunk, i, first):
        for j in range(first, group):
            peer = field_of(i) * group + (inside + j) % group
            block_copy(chunk, peer, me).start()

    def send_pair(chunk, pair, last):
        for i in range(2):
            send_field(chunk, 2 * pair + i, 1 if last and i == 1 else 0)

    def relax_and_send(pair, carry):
        relax(pair)
        send_pair(0, pair, False)
        return carry

    relax(0)
    pl.semaphore_wait(barrier, col_total - 1 + band_total - 1)
    send_pair(0, 0, False)
    lax.fori_loop(1, field_total // 2 - 1, relax_and_send, 0)
    relax(field_total // 2 - 1)
    send_pair(0, field_total // 2 - 1, True)

    def second_chunk(i, carry):
        send_field(1, i, 0)
        return carry

    lax.fori_loop(0, field_total - 1, second_chunk, 0)
    send_field(1, field_total - 1, 1)
    base_copy.wait()

    def rows_of(ref, source, chunk):
        start, size = chunks[chunk]
        values = ref[source, start : start + size].astype(jnp.float32)
        return values.reshape(size * row_total, width).astype(jnp.bfloat16)

    def accumulate(chunk, first_rows, second_rows, sources, fresh):
        start, size = chunks[chunk]
        held = slice(start * row_total, (start + size) * row_total)
        rows = jnp.concatenate([first_rows, second_rows], axis=1)
        for j in range(band_total):
            lanes = slice(j * piece_width, (j + 1) * piece_width)
            table = jnp.concatenate(
                [
                    (
                        base_buf[0, :, lanes] * phase_ref[source, 0:1, lanes]
                        + base_buf[1, :, lanes] * phase_ref[source, 1:2, lanes]
                    ).astype(jnp.bfloat16)
                    for source in sources
                ],
                axis=0,
            )
            value = jnp.dot(rows, table, preferred_element_type=jnp.float32)
            total[j, held] = value if fresh else total[j, held] + value

    def band_copy(chunk, j, to_peer):
        start, size = chunks[chunk]
        held = pl.ds(start * row_total, size * row_total)
        peer = (band + j) % band_total
        origin = band if to_peer else peer
        return pltpu.make_async_remote_copy(
            src_ref=outgoing.at[chunk, peer, held],
            dst_ref=incoming.at[chunk, origin, held],
            send_sem=band_send.at[chunk, peer],
            recv_sem=band_recv.at[chunk, origin],
            device_id={"band": peer},
            device_id_type=MESH,
        )

    mate = me + 1 - 2 * (me % 2)
    for chunk, (start, size) in enumerate(chunks):
        held = slice(start * row_total, (start + size) * row_total)
        block_copy(chunk, mate, mate).wait_recv()
        accumulate(
            chunk, rows_of(blocks, me, chunk), rows_of(landed, mate, chunk), (me, mate), True
        )

        def receive(t, carry):
            first = 2 * flip(me // 2, t, col_total // 2)
            block_copy(chunk, first, first).wait_recv()
            block_copy(chunk, first + 1, first + 1).wait_recv()
            accumulate(
                chunk, rows_of(landed, first, chunk), rows_of(landed, first + 1, chunk),
                (first, first + 1), False,
            )
            return carry

        lax.fori_loop(1, col_total // 2, receive, 0)
        for j in range(1, band_total):
            peer = (band + j) % band_total
            outgoing[chunk, peer, held] = (total[peer, held] * scale).astype(jnp.bfloat16)
        for j in range(1, band_total):
            band_copy(chunk, j, True).start()

    def put(origin, start, size, values):
        pieces = piece_width // 128
        for level in range(size):
            rows = values[level * row_total : (level + 1) * row_total]
            for k in range(pieces):
                out_ref[start + level, origin, pl.ds(k, row_total, stride=pieces), :] = rows[
                    :, k * 128 : (k + 1) * 128
                ]

    for start, size in chunks:
        held = slice(start * row_total, (start + size) * row_total)
        put(band, start, size, total[band, held] * scale)
    for chunk, (start, size) in enumerate(chunks):
        held = slice(start * row_total, (start + size) * row_total)
        for j in range(1, band_total):
            peer = (band + j) % band_total
            band_copy(chunk, j, False).wait_recv()
            put(peer, start, size, incoming[chunk, peer, held].astype(jnp.float32))

    def drain(t, carry):
        peer = (me + t) % col_total
        for chunk in range(len(chunks)):
            block_copy(chunk, peer, me).wait_send()
        return carry

    lax.fori_loop(1, col_total, drain, 0)
    for chunk in range(len(chunks)):
        for j in range(1, band_total):
            band_copy(chunk, j, True).wait_send()


def tables(width, col_total, band_total):
    length = width * col_total
    waves = np.arange(length // 4, dtype=np.int64).reshape(-1, 1, 128)
    shape = (waves.shape[0], 2, 128)
    wave_of = np.broadcast_to(waves, shape).reshape(-1)
    imaginary = np.broadcast_to(np.arange(2).reshape(1, 2, 1), shape).reshape(-1)
    angle = 2.0 * np.pi * ((np.arange(width)[:, None] * wave_of[None, :]) % length) / length
    cosine, sine = np.cos(angle), np.sin(angle)
    plain = np.where(imaginary[None, :] == 1, -sine, cosine)
    crossed = np.where(imaginary[None, :] == 1, -cosine, -sine)
    base = np.stack([plain, crossed])
    turn = 2.0 * np.pi * ((np.arange(col_total)[:, None] * wave_of[None, :]) % col_total) / col_total
    phase = np.stack([np.cos(turn), np.sin(turn)], axis=1)
    return base.astype(np.float32), phase.astype(np.float32)


def shards(fields, inverse, block_costs, row_length):
    field_total, level_total, row_total, width = fields.shape
    col_total, band_total = lax.axis_size("col"), lax.axis_size("band")
    own_levels = field_total * level_total // col_total
    vmem = pl.BlockSpec(memory_space=pltpu.VMEM)
    smem = pl.BlockSpec(memory_space=pltpu.SMEM)
    hbm = pl.BlockSpec(memory_space=pl.ANY)
    base, phase = tables(width, col_total, band_total)
    own_rows, piece_width = own_levels * row_total, base.shape[2] // band_total
    waves = piece_width // 2
    spectra = pl.pallas_call(
        functools.partial(
            spectral_kernel, col_total, band_total, 1.0 / math.sqrt(width * col_total)
        ),
        name="spectral",
        out_shape=jax.ShapeDtypeStruct((own_levels, band_total, row_total * piece_width // 128, 128), jnp.float32),
        in_specs=[smem, smem, hbm, vmem, hbm, vmem],
        out_specs=vmem,
        scratch_shapes=[
            pltpu.VMEM(fields.shape, jnp.bfloat16),
            pltpu.VMEM((2, level_total * row_total, width), jnp.float32),
            pltpu.VMEM((2, level_total * row_total, width), jnp.float32),
            pltpu.VMEM((2, level_total, row_total * width), jnp.bfloat16),
            pltpu.VMEM((col_total, own_levels, row_total, width), jnp.bfloat16),
            pltpu.VMEM((col_total, own_levels, row_total, width), jnp.bfloat16),
            pltpu.VMEM((band_total, own_rows, piece_width), jnp.float32),
            pltpu.VMEM((2, band_total, own_rows, piece_width), jnp.bfloat16),
            pltpu.VMEM((2, band_total, own_rows, piece_width), jnp.bfloat16),
            pltpu.VMEM(base.shape, jnp.float32),
            pltpu.SemaphoreType.DMA((field_total,)),
            pltpu.SemaphoreType.DMA,
            pltpu.SemaphoreType.DMA((2, col_total)),
            pltpu.SemaphoreType.DMA((2, col_total)),
            pltpu.SemaphoreType.DMA((2, band_total)),
            pltpu.SemaphoreType.DMA((2, band_total)),
        ],
        compiler_params=pltpu.CompilerParams(collective_id=0, has_side_effects=True),
    )(block_costs, row_length, fields, inverse, jnp.asarray(base), jnp.asarray(phase))
    split = spectra.reshape(own_levels, band_total * row_total, waves // 128, 2, 128)
    return split.transpose(0, 1, 3, 2, 4).reshape(own_levels, band_total * row_total, 2, waves)


def solution(mesh):
    return jax.shard_map(
        shards,
        mesh=mesh,
        in_specs=(P(None, None, "band", "col"), P(), P("col", "band"), P("band")),
        out_specs=P("col", None, None, "band"),
        check_vma=False,
    )
```

```python
import functools
import math

import jax
import jax.numpy as jnp
import numpy as np
from jax import lax
from jax.experimental import pallas as pl
from jax.experimental.pallas import tpu as pltpu
from jax.sharding import PartitionSpec as P

sweep_total = 8
MESH = pl.DeviceIdType.MESH


def flip(position, step, total):
    result, bit = 0, 1
    while bit < total:
        result = result + bit * (((position // bit) + (step // bit)) % 2)
        bit *= 2
    return result


def spectral_kernel(
    col_total, band_total, scale,
    cost_ref, length_ref, fields_ref, inverse_ref, base_ref, phase_ref, out_ref,
    fields_buf, turn_in, turn_out, state_ref, blocks, landed, total, outgoing, incoming, base_buf,
    field_sem, base_sem, send_sem, recv_sem, band_send, band_recv,
):
    me, band = lax.axis_index("col"), lax.axis_index("band")
    field_total, level_total, row_total, width = fields_buf.shape
    own_levels = landed.shape[1]
    piece_width = total.shape[2]
    group = col_total // field_total
    place, inside = me // group, me % group
    toward = 1 - 2 * (place // (field_total // 2))
    head = (3 * own_levels + 4) // 5
    chunks = ((0, head), (head, own_levels - head))

    def field_of(i):
        return (place + field_total + toward * (1 + i)) % field_total

    def field_copy(i):
        f = field_of(i)
        return pltpu.make_async_copy(fields_ref.at[f], fields_buf.at[i], field_sem.at[i])

    for i in range(field_total):
        field_copy(i).start()
    base_copy = pltpu.make_async_copy(base_ref, base_buf, base_sem)
    base_copy.start()
    barrier = pltpu.get_barrier_semaphore()

    def greet(t, carry):
        pl.semaphore_signal(
            barrier, inc=1, device_id={"col": (me + t) % col_total}, device_id_type=MESH
        )
        return carry

    lax.fori_loop(1, col_total, greet, 0)
    for j in range(1, band_total):
        pl.semaphore_signal(
            barrier, inc=1, device_id={"band": (band + j) % band_total}, device_id_type=MESH
        )

    costs = jnp.concatenate(
        [jnp.full((1, width), cost_ref[0, r], jnp.int32) for r in range(row_total)], axis=1
    )
    longitude = me * width + lax.broadcasted_iota(jnp.int32, (1, width), 1)
    keep = jnp.concatenate(
        [(longitude < length_ref[r]).astype(jnp.int32) for r in range(row_total)], axis=0
    )[None] > 0

    def relax(pair):
        for k in range(2):
            field_copy(2 * pair + k).wait()
            turn_in[k] = (
                fields_buf[2 * pair + k].astype(jnp.float32).reshape(level_total * row_total, width)
            )
        for k in range(2):
            for r in range(row_total):
                piece = turn_in[k, pl.ds(r, level_total, stride=row_total), :]
                state_ref[k, :, r * width : (r + 1) * width] = piece.astype(jnp.bfloat16)

        def sweep(s, carry):
            active = costs > s
            for k in range(2):
                before = state_ref[k]
                applied = jnp.dot(
                    inverse_ref[field_of(2 * pair + k)], before, preferred_element_type=jnp.float32
                )
                state_ref[k] = jnp.where(
                    active, applied, before.astype(jnp.float32)
                ).astype(jnp.bfloat16)
            return carry

        lax.fori_loop(0, sweep_total, sweep, 0)
        for k in range(2):
            for r in range(row_total):
                turn_out[k, pl.ds(r, level_total, stride=row_total), :] = state_ref[
                    k, :, r * width : (r + 1) * width
                ].astype(jnp.float32)
        for k in range(2):
            f = field_of(2 * pair + k)
            for q in range(group):
                rows = slice(q * own_levels * row_total, (q + 1) * own_levels * row_total)
                shape = (own_levels, row_total, width)
                initial = turn_in[k, rows, :].reshape(shape)
                tendency = (turn_out[k, rows, :].reshape(shape) - initial).astype(jnp.bfloat16)
                updated = initial + tendency.astype(jnp.float32)
                blocks[f * group + q] = jnp.where(keep, updated, 0.0).astype(jnp.bfloat16)

    def block_copy(chunk, peer, source):
        start, size = chunks[chunk]
        return pltpu.make_async_remote_copy(
            src_ref=blocks.at[peer, pl.ds(start, size)],
            dst_ref=landed.at[source, pl.ds(start, size)],
            send_sem=send_sem.at[chunk, peer],
            recv_sem=recv_sem.at[chunk, source],
            device_id={"col": peer},
            device_id_type=MESH,
        )

    def send_field(chunk, i, first):
        for j in range(first, group):
            peer = field_of(i) * group + (inside + j) % group
            block_copy(chunk, peer, me).start()

    def send_pair(chunk, pair, last):
        for i in range(2):
            send_field(chunk, 2 * pair + i, 1 if last and i == 1 else 0)

    def relax_and_send(pair, carry):
        relax(pair)
        send_pair(0, pair, False)
        return carry

    relax(0)
    pl.semaphore_wait(barrier, col_total - 1 + band_total - 1)
    send_pair(0, 0, False)
    lax.fori_loop(1, field_total // 2 - 1, relax_and_send, 0)
    relax(field_total // 2 - 1)
    send_pair(0, field_total // 2 - 1, True)

    def second_chunk(i, carry):
        send_field(1, i, 0)
        return carry

    lax.fori_loop(0, field_total - 1, second_chunk, 0)
    send_field(1, field_total - 1, 1)
    base_copy.wait()

    def rows_of(ref, source, chunk):
        start, size = chunks[chunk]
        values = ref[source, start : start + size].astype(jnp.float32)
        return values.reshape(size * row_total, width).astype(jnp.bfloat16)

    def accumulate(chunk, first_rows, second_rows, sources, fresh):
        start, size = chunks[chunk]
        held = slice(start * row_total, (start + size) * row_total)
        rows = jnp.concatenate([first_rows, second_rows], axis=1)
        for j in range(band_total):
            lanes = slice(j * piece_width, (j + 1) * piece_width)
            table = jnp.concatenate(
                [
                    (
                        base_buf[0, :, lanes] * phase_ref[source, 0:1, lanes]
                        + base_buf[1, :, lanes] * phase_ref[source, 1:2, lanes]
                    ).astype(jnp.bfloat16)
                    for source in sources
                ],
                axis=0,
            )
            value = jnp.dot(rows, table, preferred_element_type=jnp.float32)
            total[j, held] = value if fresh else total[j, held] + value

    def band_copy(chunk, j, to_peer):
        start, size = chunks[chunk]
        held = pl.ds(start * row_total, size * row_total)
        peer = (band + j) % band_total
        origin = band if to_peer else peer
        return pltpu.make_async_remote_copy(
            src_ref=outgoing.at[chunk, peer, held],
            dst_ref=incoming.at[chunk, origin, held],
            send_sem=band_send.at[chunk, peer],
            recv_sem=band_recv.at[chunk, origin],
            device_id={"band": peer},
            device_id_type=MESH,
        )

    mate = me + 1 - 2 * (me % 2)
    for chunk, (start, size) in enumerate(chunks):
        held = slice(start * row_total, (start + size) * row_total)
        block_copy(chunk, mate, mate).wait_recv()
        accumulate(
            chunk, rows_of(blocks, me, chunk), rows_of(landed, mate, chunk), (me, mate), True
        )

        def receive(t, carry):
            first = 2 * flip(me // 2, t, col_total // 2)
            block_copy(chunk, first, first).wait_recv()
            block_copy(chunk, first + 1, first + 1).wait_recv()
            accumulate(
                chunk, rows_of(landed, first, chunk), rows_of(landed, first + 1, chunk),
                (first, first + 1), False,
            )
            return carry

        lax.fori_loop(1, col_total // 2, receive, 0)
        for j in range(1, band_total):
            peer = (band + j) % band_total
            outgoing[chunk, peer, held] = (total[peer, held] * scale).astype(jnp.bfloat16)
        for j in range(1, band_total):
            band_copy(chunk, j, True).start()

    def put(origin, start, size, values):
        pieces = piece_width // 128
        for level in range(size):
            rows = values[level * row_total : (level + 1) * row_total]
            for k in range(pieces):
                out_ref[start + level, origin, pl.ds(k, row_total, stride=pieces), :] = rows[
                    :, k * 128 : (k + 1) * 128
                ]

    for start, size in chunks:
        held = slice(start * row_total, (start + size) * row_total)
        put(band, start, size, total[band, held] * scale)
    for chunk, (start, size) in enumerate(chunks):
        held = slice(start * row_total, (start + size) * row_total)
        for j in range(1, band_total):
            peer = (band + j) % band_total
            band_copy(chunk, j, False).wait_recv()
            put(peer, start, size, incoming[chunk, peer, held].astype(jnp.float32))

    def drain(t, carry):
        peer = (me + t) % col_total
        for chunk in range(len(chunks)):
            block_copy(chunk, peer, me).wait_send()
        return carry

    lax.fori_loop(1, col_total, drain, 0)
    for chunk in range(len(chunks)):
        for j in range(1, band_total):
            band_copy(chunk, j, True).wait_send()


def deliver_kernel(size, in_ref, out_ref, held, in_sem, out_sem):
    pieces = held.shape[0] // size
    parts = [pl.ds(p * size, size) for p in range(pieces)]
    reads = [
        pltpu.make_async_copy(in_ref.at[part], held.at[part], in_sem.at[p])
        for p, part in enumerate(parts)
    ]
    writes = [
        pltpu.make_async_copy(held.at[part], out_ref.at[part], out_sem.at[p])
        for p, part in enumerate(parts)
    ]
    for read in reads:
        read.start()
    for read, write in zip(reads, writes):
        read.wait()
        write.start()
    for write in writes:
        write.wait()


def tables(width, col_total, band_total):
    length = width * col_total
    waves = np.arange(length // 4, dtype=np.int64).reshape(-1, 1, 128)
    shape = (waves.shape[0], 2, 128)
    wave_of = np.broadcast_to(waves, shape).reshape(-1)
    imaginary = np.broadcast_to(np.arange(2).reshape(1, 2, 1), shape).reshape(-1)
    angle = 2.0 * np.pi * ((np.arange(width)[:, None] * wave_of[None, :]) % length) / length
    cosine, sine = np.cos(angle), np.sin(angle)
    plain = np.where(imaginary[None, :] == 1, -sine, cosine)
    crossed = np.where(imaginary[None, :] == 1, -cosine, -sine)
    base = np.stack([plain, crossed])
    turn = 2.0 * np.pi * ((np.arange(col_total)[:, None] * wave_of[None, :]) % col_total) / col_total
    phase = np.stack([np.cos(turn), np.sin(turn)], axis=1)
    return base.astype(np.float32), phase.astype(np.float32)


def shards(fields, inverse, block_costs, row_length):
    field_total, level_total, row_total, width = fields.shape
    col_total, band_total = lax.axis_size("col"), lax.axis_size("band")
    own_levels = field_total * level_total // col_total
    vmem = pl.BlockSpec(memory_space=pltpu.VMEM)
    smem = pl.BlockSpec(memory_space=pltpu.SMEM)
    hbm = pl.BlockSpec(memory_space=pl.ANY)
    base, phase = tables(width, col_total, band_total)
    own_rows, piece_width = own_levels * row_total, base.shape[2] // band_total
    waves = piece_width // 2
    spectra = pl.pallas_call(
        functools.partial(
            spectral_kernel, col_total, band_total, 1.0 / math.sqrt(width * col_total)
        ),
        name="spectral",
        out_shape=jax.ShapeDtypeStruct((own_levels, band_total, row_total * piece_width // 128, 128), jnp.float32),
        in_specs=[smem, smem, hbm, vmem, hbm, vmem],
        out_specs=vmem,
        scratch_shapes=[
            pltpu.VMEM(fields.shape, jnp.bfloat16),
            pltpu.VMEM((2, level_total * row_total, width), jnp.float32),
            pltpu.VMEM((2, level_total * row_total, width), jnp.float32),
            pltpu.VMEM((2, level_total, row_total * width), jnp.bfloat16),
            pltpu.VMEM((col_total, own_levels, row_total, width), jnp.bfloat16),
            pltpu.VMEM((col_total, own_levels, row_total, width), jnp.bfloat16),
            pltpu.VMEM((band_total, own_rows, piece_width), jnp.float32),
            pltpu.VMEM((2, band_total, own_rows, piece_width), jnp.bfloat16),
            pltpu.VMEM((2, band_total, own_rows, piece_width), jnp.bfloat16),
            pltpu.VMEM(base.shape, jnp.float32),
            pltpu.SemaphoreType.DMA((field_total,)),
            pltpu.SemaphoreType.DMA,
            pltpu.SemaphoreType.DMA((2, col_total)),
            pltpu.SemaphoreType.DMA((2, col_total)),
            pltpu.SemaphoreType.DMA((2, band_total)),
            pltpu.SemaphoreType.DMA((2, band_total)),
        ],
        compiler_params=pltpu.CompilerParams(collective_id=0, has_side_effects=True),
    )(block_costs, row_length, fields, inverse, jnp.asarray(base), jnp.asarray(phase))
    pieces = next(p for p in (5, 4, 2, 1) if own_levels % p == 0)
    spectra = pl.pallas_call(
        functools.partial(deliver_kernel, own_levels // pieces),
        name="deliver",
        out_shape=jax.ShapeDtypeStruct(spectra.shape, spectra.dtype),
        in_specs=[hbm],
        out_specs=hbm,
        scratch_shapes=[
            pltpu.VMEM(spectra.shape, spectra.dtype),
            pltpu.SemaphoreType.DMA((pieces,)),
            pltpu.SemaphoreType.DMA((pieces,)),
        ],
    )(spectra)
    split = spectra.reshape(own_levels, band_total * row_total, waves // 128, 2, 128)
    return split.transpose(0, 1, 3, 2, 4).reshape(own_levels, band_total * row_total, 2, waves)


def solution(mesh):
    return jax.shard_map(
        shards,
        mesh=mesh,
        in_specs=(P(None, None, "band", "col"), P(), P("col", "band"), P("band")),
        out_specs=P("col", None, None, "band"),
        check_vma=False,
    )
```

```python
import functools
import math

import jax
import jax.numpy as jnp
import numpy as np
from jax import lax
from jax.experimental import pallas as pl
from jax.experimental.pallas import tpu as pltpu
from jax.sharding import PartitionSpec as P

sweep_total = 8
MESH = pl.DeviceIdType.MESH


def flip(position, step, total):
    result, bit = 0, 1
    while bit < total:
        result = result + bit * (((position // bit) + (step // bit)) % 2)
        bit *= 2
    return result


def spectral_kernel(
    col_total, band_total, scale,
    cost_ref, length_ref, fields_ref, inverse_ref, base_ref, phase_ref, out_ref,
    fields_buf, turn_in, turn_out, state_ref, blocks, landed, total, outgoing, incoming, base_buf,
    field_sem, base_sem, send_sem, recv_sem, band_send, band_recv,
):
    me, band = lax.axis_index("col"), lax.axis_index("band")
    field_total, level_total, row_total, width = fields_buf.shape
    own_levels = landed.shape[1]
    piece_width = total.shape[2]
    group = col_total // field_total
    place, inside = me // group, me % group
    toward = 1 - 2 * (place // (field_total // 2))
    head = (3 * own_levels + 4) // 5
    chunks = ((0, head), (head, own_levels - head))

    def field_of(i):
        return (place + field_total + toward * (1 + i)) % field_total

    def field_copy(i):
        f = field_of(i)
        return pltpu.make_async_copy(fields_ref.at[f], fields_buf.at[i], field_sem.at[i])

    for i in range(field_total):
        field_copy(i).start()
    base_copy = pltpu.make_async_copy(base_ref, base_buf, base_sem)
    base_copy.start()
    barrier = pltpu.get_barrier_semaphore()

    def greet(t, carry):
        pl.semaphore_signal(
            barrier, inc=1, device_id={"col": (me + t) % col_total}, device_id_type=MESH
        )
        return carry

    lax.fori_loop(1, col_total, greet, 0)
    for j in range(1, band_total):
        pl.semaphore_signal(
            barrier, inc=1, device_id={"band": (band + j) % band_total}, device_id_type=MESH
        )

    costs = jnp.concatenate(
        [jnp.full((1, width), cost_ref[0, r], jnp.int32) for r in range(row_total)], axis=1
    )
    longitude = me * width + lax.broadcasted_iota(jnp.int32, (1, width), 1)
    keep = jnp.concatenate(
        [(longitude < length_ref[r]).astype(jnp.int32) for r in range(row_total)], axis=0
    )[None] > 0

    def relax(pair):
        for k in range(2):
            field_copy(2 * pair + k).wait()
            turn_in[k] = (
                fields_buf[2 * pair + k].astype(jnp.float32).reshape(level_total * row_total, width)
            )
        for k in range(2):
            for r in range(row_total):
                piece = turn_in[k, pl.ds(r, level_total, stride=row_total), :]
                state_ref[k, :, r * width : (r + 1) * width] = piece.astype(jnp.bfloat16)

        def sweep(s, carry):
            active = costs > s
            for k in range(2):
                before = state_ref[k]
                applied = jnp.dot(
                    inverse_ref[field_of(2 * pair + k)], before, preferred_element_type=jnp.float32
                )
                state_ref[k] = jnp.where(
                    active, applied, before.astype(jnp.float32)
                ).astype(jnp.bfloat16)
            return carry

        lax.fori_loop(0, sweep_total, sweep, 0, unroll=True)
        for k in range(2):
            for r in range(row_total):
                turn_out[k, pl.ds(r, level_total, stride=row_total), :] = state_ref[
                    k, :, r * width : (r + 1) * width
                ].astype(jnp.float32)
        for k in range(2):
            f = field_of(2 * pair + k)
            for q in range(group):
                rows = slice(q * own_levels * row_total, (q + 1) * own_levels * row_total)
                shape = (own_levels, row_total, width)
                initial = turn_in[k, rows, :].reshape(shape)
                tendency = (turn_out[k, rows, :].reshape(shape) - initial).astype(jnp.bfloat16)
                updated = initial + tendency.astype(jnp.float32)
                blocks[f * group + q] = jnp.where(keep, updated, 0.0).astype(jnp.bfloat16)

    def block_copy(chunk, peer, source):
        start, size = chunks[chunk]
        return pltpu.make_async_remote_copy(
            src_ref=blocks.at[peer, pl.ds(start, size)],
            dst_ref=landed.at[source, pl.ds(start, size)],
            send_sem=send_sem.at[chunk, peer],
            recv_sem=recv_sem.at[chunk, source],
            device_id={"col": peer},
            device_id_type=MESH,
        )

    def send_field(chunk, i, first):
        for j in range(first, group):
            peer = field_of(i) * group + (inside + j) % group
            block_copy(chunk, peer, me).start()

    def send_pair(chunk, pair, last):
        for i in range(2):
            send_field(chunk, 2 * pair + i, 1 if last and i == 1 else 0)

    def relax_and_send(pair, carry):
        relax(pair)
        send_pair(0, pair, False)
        return carry

    relax(0)
    pl.semaphore_wait(barrier, col_total - 1 + band_total - 1)
    send_pair(0, 0, False)
    lax.fori_loop(1, field_total // 2 - 1, relax_and_send, 0)
    relax(field_total // 2 - 1)
    send_pair(0, field_total // 2 - 1, True)

    def second_chunk(i, carry):
        send_field(1, i, 0)
        return carry

    lax.fori_loop(0, field_total - 1, second_chunk, 0)
    send_field(1, field_total - 1, 1)
    base_copy.wait()

    def rows_of(ref, source, chunk):
        start, size = chunks[chunk]
        values = ref[source, start : start + size].astype(jnp.float32)
        return values.reshape(size * row_total, width).astype(jnp.bfloat16)

    def accumulate(chunk, first_rows, second_rows, sources, fresh):
        start, size = chunks[chunk]
        held = slice(start * row_total, (start + size) * row_total)
        rows = jnp.concatenate([first_rows, second_rows], axis=1)
        for j in range(band_total):
            lanes = slice(j * piece_width, (j + 1) * piece_width)
            table = jnp.concatenate(
                [
                    (
                        base_buf[0, :, lanes] * phase_ref[source, 0:1, lanes]
                        + base_buf[1, :, lanes] * phase_ref[source, 1:2, lanes]
                    ).astype(jnp.bfloat16)
                    for source in sources
                ],
                axis=0,
            )
            value = jnp.dot(rows, table, preferred_element_type=jnp.float32)
            total[j, held] = value if fresh else total[j, held] + value

    def band_copy(chunk, j, to_peer):
        start, size = chunks[chunk]
        held = pl.ds(start * row_total, size * row_total)
        peer = (band + j) % band_total
        origin = band if to_peer else peer
        return pltpu.make_async_remote_copy(
            src_ref=outgoing.at[chunk, peer, held],
            dst_ref=incoming.at[chunk, origin, held],
            send_sem=band_send.at[chunk, peer],
            recv_sem=band_recv.at[chunk, origin],
            device_id={"band": peer},
            device_id_type=MESH,
        )

    mate = me + 1 - 2 * (me % 2)
    for chunk, (start, size) in enumerate(chunks):
        held = slice(start * row_total, (start + size) * row_total)
        block_copy(chunk, mate, mate).wait_recv()
        accumulate(
            chunk, rows_of(blocks, me, chunk), rows_of(landed, mate, chunk), (me, mate), True
        )

        def receive(t, carry):
            first = 2 * flip(me // 2, t, col_total // 2)
            block_copy(chunk, first, first).wait_recv()
            block_copy(chunk, first + 1, first + 1).wait_recv()
            accumulate(
                chunk, rows_of(landed, first, chunk), rows_of(landed, first + 1, chunk),
                (first, first + 1), False,
            )
            return carry

        lax.fori_loop(1, col_total // 2, receive, 0)
        for j in range(1, band_total):
            peer = (band + j) % band_total
            outgoing[chunk, peer, held] = (total[peer, held] * scale).astype(jnp.bfloat16)
        for j in range(1, band_total):
            band_copy(chunk, j, True).start()

    def put(origin, start, size, values):
        pieces = piece_width // 128
        for level in range(size):
            rows = values[level * row_total : (level + 1) * row_total]
            for k in range(pieces):
                out_ref[start + level, origin, pl.ds(k, row_total, stride=pieces), :] = rows[
                    :, k * 128 : (k + 1) * 128
                ]

    for start, size in chunks:
        held = slice(start * row_total, (start + size) * row_total)
        put(band, start, size, total[band, held] * scale)
    for chunk, (start, size) in enumerate(chunks):
        held = slice(start * row_total, (start + size) * row_total)
        for j in range(1, band_total):
            peer = (band + j) % band_total
            band_copy(chunk, j, False).wait_recv()
            put(peer, start, size, incoming[chunk, peer, held].astype(jnp.float32))

    def drain(t, carry):
        peer = (me + t) % col_total
        for chunk in range(len(chunks)):
            block_copy(chunk, peer, me).wait_send()
        return carry

    lax.fori_loop(1, col_total, drain, 0)
    for chunk in range(len(chunks)):
        for j in range(1, band_total):
            band_copy(chunk, j, True).wait_send()


def deliver_kernel(size, in_ref, out_ref, held, in_sem, out_sem):
    pieces = held.shape[0] // size
    parts = [pl.ds(p * size, size) for p in range(pieces)]
    reads = [
        pltpu.make_async_copy(in_ref.at[part], held.at[part], in_sem.at[p])
        for p, part in enumerate(parts)
    ]
    writes = [
        pltpu.make_async_copy(held.at[part], out_ref.at[part], out_sem.at[p])
        for p, part in enumerate(parts)
    ]
    for read in reads:
        read.start()
    for read, write in zip(reads, writes):
        read.wait()
        write.start()
    for write in writes:
        write.wait()


def tables(width, col_total, band_total):
    length = width * col_total
    waves = np.arange(length // 4, dtype=np.int64).reshape(-1, 1, 128)
    shape = (waves.shape[0], 2, 128)
    wave_of = np.broadcast_to(waves, shape).reshape(-1)
    imaginary = np.broadcast_to(np.arange(2).reshape(1, 2, 1), shape).reshape(-1)
    angle = 2.0 * np.pi * ((np.arange(width)[:, None] * wave_of[None, :]) % length) / length
    cosine, sine = np.cos(angle), np.sin(angle)
    plain = np.where(imaginary[None, :] == 1, -sine, cosine)
    crossed = np.where(imaginary[None, :] == 1, -cosine, -sine)
    base = np.stack([plain, crossed])
    turn = 2.0 * np.pi * ((np.arange(col_total)[:, None] * wave_of[None, :]) % col_total) / col_total
    phase = np.stack([np.cos(turn), np.sin(turn)], axis=1)
    return base.astype(np.float32), phase.astype(np.float32)


def shards(fields, inverse, block_costs, row_length):
    field_total, level_total, row_total, width = fields.shape
    col_total, band_total = lax.axis_size("col"), lax.axis_size("band")
    own_levels = field_total * level_total // col_total
    vmem = pl.BlockSpec(memory_space=pltpu.VMEM)
    smem = pl.BlockSpec(memory_space=pltpu.SMEM)
    hbm = pl.BlockSpec(memory_space=pl.ANY)
    base, phase = tables(width, col_total, band_total)
    own_rows, piece_width = own_levels * row_total, base.shape[2] // band_total
    waves = piece_width // 2
    spectra = pl.pallas_call(
        functools.partial(
            spectral_kernel, col_total, band_total, 1.0 / math.sqrt(width * col_total)
        ),
        name="spectral",
        out_shape=jax.ShapeDtypeStruct((own_levels, band_total, row_total * piece_width // 128, 128), jnp.float32),
        in_specs=[smem, smem, hbm, vmem, hbm, vmem],
        out_specs=vmem,
        scratch_shapes=[
            pltpu.VMEM(fields.shape, jnp.bfloat16),
            pltpu.VMEM((2, level_total * row_total, width), jnp.float32),
            pltpu.VMEM((2, level_total * row_total, width), jnp.float32),
            pltpu.VMEM((2, level_total, row_total * width), jnp.bfloat16),
            pltpu.VMEM((col_total, own_levels, row_total, width), jnp.bfloat16),
            pltpu.VMEM((col_total, own_levels, row_total, width), jnp.bfloat16),
            pltpu.VMEM((band_total, own_rows, piece_width), jnp.float32),
            pltpu.VMEM((2, band_total, own_rows, piece_width), jnp.bfloat16),
            pltpu.VMEM((2, band_total, own_rows, piece_width), jnp.bfloat16),
            pltpu.VMEM(base.shape, jnp.float32),
            pltpu.SemaphoreType.DMA((field_total,)),
            pltpu.SemaphoreType.DMA,
            pltpu.SemaphoreType.DMA((2, col_total)),
            pltpu.SemaphoreType.DMA((2, col_total)),
            pltpu.SemaphoreType.DMA((2, band_total)),
            pltpu.SemaphoreType.DMA((2, band_total)),
        ],
        compiler_params=pltpu.CompilerParams(collective_id=0, has_side_effects=True),
    )(block_costs, row_length, fields, inverse, jnp.asarray(base), jnp.asarray(phase))
    pieces = next(p for p in (5, 4, 2, 1) if own_levels % p == 0)
    spectra = pl.pallas_call(
        functools.partial(deliver_kernel, own_levels // pieces),
        name="deliver",
        out_shape=jax.ShapeDtypeStruct(spectra.shape, spectra.dtype),
        in_specs=[hbm],
        out_specs=hbm,
        scratch_shapes=[
            pltpu.VMEM(spectra.shape, spectra.dtype),
            pltpu.SemaphoreType.DMA((pieces,)),
            pltpu.SemaphoreType.DMA((pieces,)),
        ],
    )(spectra)
    split = spectra.reshape(own_levels, band_total * row_total, waves // 128, 2, 128)
    return split.transpose(0, 1, 3, 2, 4).reshape(own_levels, band_total * row_total, 2, waves)


def solution(mesh):
    return jax.shard_map(
        shards,
        mesh=mesh,
        in_specs=(P(None, None, "band", "col"), P(), P("col", "band"), P("band")),
        out_specs=P("col", None, None, "band"),
        check_vma=False,
    )
```
